32 devices in a mesh: neur: 4 (over z), tri: 4 (over y, x), bin: 2 (over core).
Axes of the slice: x: 2, y: 2, z: 4, core: 2. Of those that a mesh axis runs over, the one named last changes fastest.
Arguments:
- tensor: bfloat16 [2048, 128, 256], P('neur', 'tri', 'bin'), may hold values from -3600 to 3600
- bin_factor: bfloat16 [256, 64], P('bin'), may hold values from 0.049804688 to 1
- trial_factor: bfloat16 [128, 64], P('tri'), may hold values from 0.049804688 to 1
Outputs:
- neuron_factor: float32 [2048, 64], P(('neur', 'tri', 'bin'))
- weights: float32 [64], replicated
The draws below stay inside these ranges and needn't reach their ends.
All inputs are finite; a program needn't handle non-finite values.
Results may differ from the reference program's by a relative error of at most 0.0003.
Values sent between devices are 32-bit elements; how exact they have to be, the bound alone decides.
No kernel may reach another device: no remote copies, remote signals or barrier semaphores. Data moves between devices by JAX's collectives and lax.ppermute only.
A program may use at most 64 MiB of HBM per device.

```python
import jax
import jax.numpy as jnp
from jax import lax

ROWS_DEV = 512
TRIALS = 128
BINS = 256
RANK = 64
NEURONS = 2048
N_NEUR = 4


def draw_tensor(key, part):
    key_noise = jax.random.fold_in(key, 11)
    key_rows = jax.random.fold_in(key, 12)
    key_bins = jax.random.fold_in(key, 13)
    shape = (NEURONS, TRIALS, BINS)
    noise = jnp.clip(jax.random.normal(key_noise, shape, jnp.float32), -6.0, 6.0)
    position = jnp.arange(NEURONS, dtype=jnp.float32) / NEURONS
    row_scale = 10.0 ** (0.5 * position + 0.5 * jax.random.uniform(key_rows, (NEURONS,), jnp.float32))
    bin_scale = 10.0 ** jax.random.uniform(key_bins, (BINS,), jnp.float32)
    values = 6.0 * noise * row_scale[:, None, None] * bin_scale[None, None, :]
    return values.astype(jnp.bfloat16)


def steps_of(rng, dims, split, least, top_value):
    factor_of, own = 1.0, jax.random.fold_in(rng, 6)
    for dim, shards_of in split:
        steps = jnp.exp(jax.random.uniform(jax.random.fold_in(own, dim), (shards_of,), jnp.float32, least / len(split), top_value / len(split)))
        factor_of = factor_of * jnp.repeat(steps, dims[dim] // shards_of).reshape([-1 if axis == dim else 1 for axis in range(len(dims))])
    return factor_of


def setup_inputs(seed: int = 0) -> dict:
    arg_keys = jax.random.split(jax.random.key(seed), 4)
    tensor = draw_tensor(jax.random.fold_in(arg_keys[3], 71), 0)
    bin_factor = jnp.clip(0.049804688 + 0.9501953 * jax.random.uniform(arg_keys[1], (BINS, RANK), jnp.float32) ** steps_of(arg_keys[1], (BINS, RANK), ((0, 2),), -0.2, 0.2), 0.049804688, 1.0).astype(jnp.bfloat16)
    trial_factor = jnp.clip(0.049804688 + 0.9501953 * jax.random.uniform(arg_keys[2], (TRIALS, RANK), jnp.float32) ** steps_of(arg_keys[2], (TRIALS, RANK), ((0, 4),), -0.2, 0.2), 0.049804688, 1.0).astype(jnp.bfloat16)
    return dict(tensor=tensor, bin_factor=bin_factor, trial_factor=trial_factor)


def reference(tensor, bin_factor, trial_factor):
    trial_wide = trial_factor.astype(jnp.float32)

    def block_product(block):
        count = block.shape[0]
        section = jnp.dot(block.reshape(count * TRIALS, BINS).astype(jnp.float32), bin_factor.astype(jnp.float32), preferred_element_type=jnp.float32)
        section = section.reshape(count, TRIALS, RANK)
        return lax.optimization_barrier(jnp.sum(section * trial_wide[None], axis=1))
    blocks = tensor.reshape(N_NEUR, ROWS_DEV, TRIALS, BINS)
    mttkrp = lax.map(block_product, blocks).reshape(NEURONS, RANK)
    gram = jnp.dot(bin_factor.T.astype(jnp.float32), bin_factor.astype(jnp.float32), preferred_element_type=jnp.float32)
    gram = gram * jnp.dot(trial_factor.T.astype(jnp.float32), trial_factor.astype(jnp.float32), preferred_element_type=jnp.float32)
    lower = jnp.linalg.cholesky(gram)
    solved = jax.scipy.linalg.cho_solve((lower, True), mttkrp.T).T
    mean_square = lax.optimization_barrier(jnp.mean(solved * solved, axis=0))
    weights = jnp.sqrt(mean_square + 1e-06)
    return (solved / weights, weights)
```

```python
import functools

import jax
import jax.numpy as jnp
from jax import lax
from jax.experimental import pallas as pl
from jax.experimental.pallas import tpu as pltpu
from jax.sharding import PartitionSpec as P

SUB = 8
EXACT = lax.Precision.HIGHEST


def parity(index, count):
    result = index & 1
    for bit in range(1, count.bit_length() - 1):
        result = result ^ ((index >> bit) & 1)
    return result


def gram_of(factor_t):
    return lax.dot_general(factor_t, factor_t, (((1,), (1,)), ((), ())), preferred_element_type=jnp.float32)


def product_kernel(send_gram, half_ref, tensor_ref, bin_t_ref, trial_ref, out_ref, wide_ref):
    step = pl.program_id(0)
    rows, trials, bins = tensor_ref.shape
    rank = bin_t_ref.shape[0]
    pair = trials // 2

    @pl.when(step == 0)
    def _():
        bin_t = bin_t_ref[...]
        zero = jnp.zeros_like(bin_t)
        wide_ref[:rank, :bins] = bin_t
        wide_ref[:rank, bins:] = zero
        wide_ref[rank:, :bins] = zero
        wide_ref[rank:, bins:] = bin_t
        top = rows * pl.num_programs(0)
        if send_gram:
            out_ref[pl.ds(top, rank), :] = gram_of(bin_t)
        else:
            trial = trial_ref[...]
            out_ref[pl.ds(top, rank), :] = lax.dot_general(trial, trial, (((0,), (0,)), ((), ())), preferred_element_type=jnp.float32)

    trial = trial_ref[...].astype(jnp.float32)
    trial = jnp.concatenate([trial[:pair], trial[pair:]], axis=1)
    low = tensor_ref[:, :pair, :].reshape(rows * pair, bins)
    high = tensor_ref[:, pair:, :].reshape(rows * pair, bins)
    section = lax.dot_general(
        jnp.concatenate([low, high], axis=1), wide_ref[...], (((1,), (1,)), ((), ())), preferred_element_type=jnp.float32
    )
    total = jnp.sum(section.reshape(rows, pair, 2 * rank) * trial[None], axis=1)
    out_ref[pl.ds(pl.multiple_of(step * rows, SUB), rows), :] = total[:, :rank] + total[:, rank:]


def products(tensor, bin_t, trial_factor, half, steps, send_gram):
    neurons, trials, bins = tensor.shape
    rank = bin_t.shape[0]
    rows = neurons // (2 * steps)
    return pl.pallas_call(
        functools.partial(product_kernel, send_gram),
        grid_spec=pltpu.PrefetchScalarGridSpec(
            num_scalar_prefetch=1,
            grid=(steps,),
            in_specs=[
                pl.BlockSpec((rows, trials, bins), lambda t, half: (2 * t + (half[0] ^ parity(t, steps)), 0, 0)),
                pl.BlockSpec((rank, bins), lambda t, half: (0, 0)),
                pl.BlockSpec((trials, rank), lambda t, half: (0, 0)),
            ],
            out_specs=pl.BlockSpec((rows * steps + rank, rank), lambda t, half: (0, 0)),
            scratch_shapes=[pltpu.VMEM((2 * rank, 2 * bins), jnp.bfloat16)],
        ),
        out_shape=jax.ShapeDtypeStruct((rows * steps + rank, rank), jnp.float32),
        name="products",
    )(half, tensor, bin_t, trial_factor)


def inverse_tiles(tiles):
    shape = tiles[0].shape
    count = len(tiles)
    lane = lax.broadcasted_iota(jnp.int32, shape, 1)
    sub = lax.broadcasted_iota(jnp.int32, shape, 0)
    across = lambda tile, j: jnp.broadcast_to(tile[:, j : j + 1], shape)
    down = lambda tile, i: jnp.broadcast_to(tile[i : i + 1, :], shape)
    for panel in range(count):
        base = panel * SUB
        columns = [across(tiles[panel], base + j) for j in range(SUB)]
        block = tiles[panel]
        for k in range(SUB):
            scale = 1.0 / down(columns[k], k)
            column = columns[k]
            row = jnp.where(lane == base + k, 1.0, down(block, k)) * scale
            block = jnp.where(sub == k, row, jnp.where(lane == base + k, 0.0, block) - column * row)
            for j in range(k + 1, SUB):
                row = down(columns[j], k) * scale
                columns[j] = jnp.where(sub == k, row, columns[j] - column * row)
        inside = (lane >= base) & (lane < base + SUB)
        rows = [down(block, j) for j in range(SUB)]
        updated = {panel: block}
        for index in range(1, count):
            index = (panel + index) % count
            tile = tiles[index]
            even = across(tile, base) * rows[0]
            odd = jnp.where(inside, 0.0, tile)
            for j in range(1, SUB):
                if j % 2:
                    odd = odd - across(tile, base + j) * rows[j]
                else:
                    even = even + across(tile, base + j) * rows[j]
            updated[index] = odd - even
        tiles = [updated[index] for index in range(count)]
    return tiles


def inverse_kernel(bin_a_ref, bin_b_ref, trial_a_ref, trial_b_ref, out_ref):
    rank = out_ref.shape[0]
    gram = (bin_a_ref[...] + bin_b_ref[...]) * (trial_a_ref[...] + trial_b_ref[...])
    tiles = [gram[i : i + SUB, :] for i in range(0, rank, SUB)]
    for i, tile in enumerate(inverse_tiles(tiles)):
        out_ref[i * SUB : (i + 1) * SUB, :] = tile


def solve_kernel(own_ref, other_ref, inverse_ref, solved_ref, squares_ref):
    solved = jnp.dot(own_ref[...] + other_ref[...], inverse_ref[...], preferred_element_type=jnp.float32, precision=EXACT)
    solved_ref[...] = solved
    squares_ref[...] = jnp.broadcast_to(jnp.sum(solved * solved, axis=0, keepdims=True), squares_ref.shape)


def local(neur, tri, tensor, bin_factor, trial_factor):
    axes = ("neur", "tri", "bin")
    rank = bin_factor.shape[1]

    def swap(value, n, t, b):
        flat = lambda i, j, k: (i * tri + j) * 2 + k
        pairs = [(flat(i, j, k), flat(i ^ n, j ^ t, k ^ b)) for i in range(neur) for j in range(tri) for k in range(2)]
        return lax.ppermute(value, axes, pairs)

    rows = tensor.shape[0]
    share = rows // (2 * tri)
    place = lax.axis_index("tri")
    half = (lax.axis_index("bin") ^ parity(place, tri)).astype(jnp.int32)
    bin_t = bin_factor.T
    sent = products(tensor, bin_t, trial_factor, (1 - half)[None], tri, True)
    got = swap(sent, 0, 0, 1)
    own = products(tensor, bin_t, trial_factor, half[None], tri, False)
    bin_a, bin_b = sent[share * tri :], got[share * tri :]
    block = own[: share * tri] + got[: share * tri]
    trial_gram = own[share * tri :]
    bit = 1
    while bit < tri // 2:
        joined = jnp.concatenate([block, trial_gram], axis=0)
        joined = joined + swap(joined, 0, bit, 1)
        block, trial_gram = joined[: share * tri], joined[share * tri :]
        bit *= 2
    trial_other = swap(trial_gram, 0, bit, 1)
    trial_gram, block = lax.optimization_barrier((trial_gram, block))
    other = swap(block, 0, bit, 1)
    f32 = jnp.float32
    inverse = pl.pallas_call(inverse_kernel, out_shape=jax.ShapeDtypeStruct((rank, rank), f32), name="inverse")(
        bin_a, bin_b, trial_gram, trial_other
    )
    solved, squares = pl.pallas_call(
        solve_kernel,
        out_shape=(jax.ShapeDtypeStruct((share * tri, rank), f32), jax.ShapeDtypeStruct((SUB, rank), f32)),
        name="solve",
    )(block, other, inverse)
    squares = squares + swap(squares, 0, 0, 1)
    bit = 1
    while bit < neur:
        if bit * 2 < neur:
            one, two, three = (swap(squares, k * bit, 0, 1) for k in (1, 2, 3))
            squares = (squares + one) + (two + three)
            bit *= 4
        else:
            squares = squares + swap(squares, bit, 0, 1)
            bit *= 2
    weights = jnp.sqrt(squares[0] / (rows * neur) + 1e-06)
    mine = lax.dynamic_slice_in_dim(solved, place * share, share, 0)
    return (mine / weights, weights)


def solution(mesh):
    return jax.shard_map(
        functools.partial(local, mesh.shape["neur"], mesh.shape["tri"]),
        mesh=mesh,
        in_specs=(P("neur", "tri", "bin"), P("bin", None), P("tri", None)),
        out_specs=(P(("neur", "tri", "bin"), None), P()),
        check_vma=False,
    )
```

```python
import functools

import jax
import jax.numpy as jnp
from jax import lax
from jax.experimental import pallas as pl
from jax.experimental.pallas import tpu as pltpu
from jax.sharding import PartitionSpec as P

SUB = 8
EXACT = lax.Precision.HIGHEST


def held_in(*values):
    return [pltpu.with_memory_space_constraint(value, pltpu.VMEM) for value in values]


def parity(index, count):
    result = index & 1
    for bit in range(1, count.bit_length() - 1):
        result = result ^ ((index >> bit) & 1)
    return result


def gram_of(factor_t):
    return lax.dot_general(factor_t, factor_t, (((1,), (1,)), ((), ())), preferred_element_type=jnp.float32)


def packed(value):
    count = value.shape[0] // 2
    return jnp.concatenate([value[:count], value[count:]], axis=1)


def product_kernel(
    tri, tensor_ref, bin_t_ref, trial_ref, send_ref, own_ref, gram_ref, block_ref, bin_ref, local_ref, wide_ref, sems
):
    neurons, trials, bins = block_ref.shape
    rank = bin_ref.shape[0]
    pair = trials // 2
    share = neurons // (2 * tri)
    rows = share // 2
    bin_copy = pltpu.make_async_copy(bin_t_ref, bin_ref, sems.at[0])
    trial_copy = pltpu.make_async_copy(trial_ref, local_ref, sems.at[1])
    block_copy = pltpu.make_async_copy(tensor_ref, block_ref, sems.at[2])
    bin_copy.start()
    trial_copy.start()
    block_copy.start()
    half = lax.axis_index("bin") ^ parity(lax.axis_index("tri"), tri)
    bin_copy.wait()
    bin_t = bin_ref[...]
    gram = lax.dot_general(bin_t, bin_t, (((1,), (1,)), ((), ())), preferred_element_type=jnp.float32)
    send_ref[rows * tri :, :] = packed(gram)
    factor = bin_t.T
    zero = jnp.zeros_like(factor)
    wide_ref[:bins, :] = jnp.concatenate([factor, zero], axis=1)
    wide_ref[bins:, :] = jnp.concatenate([zero, factor], axis=1)
    trial_copy.wait()
    trial = local_ref[...]
    gram = lax.dot_general(trial, trial, (((0,), (0,)), ((), ())), preferred_element_type=jnp.float32)
    gram_ref[...] = packed(gram)
    trial = packed(trial.astype(jnp.float32))
    left = lax.broadcasted_iota(jnp.int32, (rows, 2 * rank), 1) < rank
    wide = wide_ref[...]
    block_copy.wait()
    for t in range(tri):
        for out_ref, side in ((send_ref, 1), (own_ref, 0)):
            first = (2 * t + (half ^ parity(t, tri) ^ side)) * share
            part = block_ref.at[pl.ds(first, share)]
            low = part[:, :pair, :].reshape(share * pair, bins)
            high = part[:, pair:, :].reshape(share * pair, bins)
            section = jnp.dot(jnp.concatenate([low, high], axis=1), wide, preferred_element_type=jnp.float32)
            total = jnp.sum(section.reshape(share, pair, 2 * rank) * trial[None], axis=1)
            total = total + pltpu.roll(total, rank, 1)
            out_ref[t * rows : (t + 1) * rows, :] = jnp.where(left, total[:rows], total[rows:])


def products(tri, tensor, bin_t, trial_factor):
    neurons, trials, bins = tensor.shape
    rank = bin_t.shape[0]
    rows = neurons // 4
    f32 = jnp.float32
    anywhere = pl.BlockSpec(memory_space=pl.ANY)
    inside = pl.BlockSpec(memory_space=pltpu.VMEM)
    return pl.pallas_call(
        functools.partial(product_kernel, tri),
        in_specs=[anywhere] * 3,
        out_specs=(inside,) * 3,
        out_shape=(
            pltpu.VMEM((rows + rank // 2, 2 * rank), f32),
            pltpu.VMEM((rows, 2 * rank), f32),
            pltpu.VMEM((rank // 2, 2 * rank), f32),
        ),
        scratch_shapes=[
            pltpu.VMEM((neurons, trials, bins), jnp.bfloat16),
            pltpu.VMEM((rank, bins), jnp.bfloat16),
            pltpu.VMEM((trials, rank), jnp.bfloat16),
            pltpu.VMEM((2 * bins, 2 * rank), jnp.bfloat16),
            pltpu.SemaphoreType.DMA((3,)),
        ],
        name="products",
    )(tensor, bin_t, trial_factor)


def inverse_tiles(tiles):
    shape = tiles[0].shape
    count = len(tiles)
    lane = lax.broadcasted_iota(jnp.int32, shape, 1)
    sub = lax.broadcasted_iota(jnp.int32, shape, 0)
    across = lambda tile, j: jnp.broadcast_to(tile[:, j : j + 1], shape)
    down = lambda tile, i: jnp.broadcast_to(tile[i : i + 1, :], shape)
    for panel in range(count):
        base = panel * SUB
        columns = [across(tiles[panel], base + j) for j in range(SUB)]
        block = tiles[panel]
        for k in range(SUB):
            scale = 1.0 / down(columns[k], k)
            column = columns[k]
            row = jnp.where(lane == base + k, 1.0, down(block, k)) * scale
            block = jnp.where(sub == k, row, jnp.where(lane == base + k, 0.0, block) - column * row)
            for j in range(k + 1, SUB):
                row = down(columns[j], k) * scale
                columns[j] = jnp.where(sub == k, row, columns[j] - column * row)
        inside = (lane >= base) & (lane < base + SUB)
        rows = [down(block, j) for j in range(SUB)]
        updated = {panel: block}
        for index in range(1, count):
            index = (panel + index) % count
            tile = tiles[index]
            even = across(tile, base) * rows[0]
            odd = jnp.where(inside, 0.0, tile)
            for j in range(1, SUB):
                if j % 2:
                    odd = odd - across(tile, base + j) * rows[j]
                else:
                    even = even + across(tile, base + j) * rows[j]
            updated[index] = odd - even
        tiles = [updated[index] for index in range(count)]
    return tiles


def inverse_kernel(bin_a_ref, bin_b_ref, trial_a_ref, trial_b_ref, out_ref):
    rank = out_ref.shape[0] // 2
    gram = (bin_a_ref[...] + bin_b_ref[...]) * (trial_a_ref[...] + trial_b_ref[...])
    tiles = [gram[i : i + SUB, lane : lane + rank] for lane in (0, rank) for i in range(0, rank // 2, SUB)]
    zero = jnp.zeros_like(tiles[0])
    for i, tile in enumerate(inverse_tiles(tiles)):
        out_ref[i * SUB : (i + 1) * SUB, :] = jnp.concatenate([tile, zero], axis=1)
        out_ref[rank + i * SUB : rank + (i + 1) * SUB, :] = jnp.concatenate([zero, tile], axis=1)


def solve_kernel(own_ref, other_ref, inverse_ref, solved_ref, squares_ref):
    rank = inverse_ref.shape[0] // 2
    solved = jnp.dot(own_ref[...] + other_ref[...], inverse_ref[...], preferred_element_type=jnp.float32, precision=EXACT)
    solved_ref[...] = solved
    squares = jnp.sum(solved * solved, axis=0, keepdims=True)
    squares = jnp.broadcast_to(squares, squares_ref.shape)
    squares_ref[...] = squares + pltpu.roll(squares, rank, 1)


def scale_kernel(count, solved_ref, one_ref, two_ref, three_ref, four_ref, out_ref, weights_ref):
    share, rank = out_ref.shape
    rows = share // 2
    squares = (one_ref[...] + two_ref[...]) + (three_ref[...] + four_ref[...])
    weights = jnp.sqrt(squares[:1] / count + 1e-06)
    weights_ref[...] = weights[:, :rank]
    mine = solved_ref[pl.ds(pl.multiple_of(lax.axis_index("tri") * rows, SUB), rows), :] / weights
    out_ref[:rows, :] = mine[:, :rank]
    out_ref[rows:, :] = mine[:, rank:]


def local(neur, tri, tensor, bin_factor, trial_factor):
    axes = ("neur", "tri", "bin")
    rank = bin_factor.shape[1]
    f32 = jnp.float32

    def swap(value, n, t, b):
        flat = lambda i, j, k: (i * tri + j) * 2 + k
        pairs = [(flat(i, j, k), flat(i ^ n, j ^ t, k ^ b)) for i in range(neur) for j in range(tri) for k in range(2)]
        return lax.ppermute(value, axes, pairs)

    rows = tensor.shape[0]
    held = rows // 4
    share = rows // (2 * tri)
    sent, own, trial_gram = products(tri, tensor, bin_factor.T, trial_factor)
    got = swap(sent, 0, 0, 1)
    bin_a, bin_b = sent[held:], got[held:]
    block = own + got[:held]
    bit = 1
    while bit < tri // 2:
        joined = jnp.concatenate([block, trial_gram], axis=0)
        joined = joined + swap(joined, 0, bit, 1)
        block, trial_gram = joined[:held], joined[held:]
        bit *= 2
    trial_other = swap(trial_gram, 0, bit, 1)
    other = swap(block, 0, bit, 1)
    inside = pl.BlockSpec(memory_space=pltpu.VMEM)
    inverse = pl.pallas_call(
        inverse_kernel,
        in_specs=[inside] * 4,
        out_specs=inside,
        out_shape=pltpu.VMEM((2 * rank, 2 * rank), f32),
        name="inverse",
    )(*held_in(bin_a, bin_b, trial_gram, trial_other))
    solved, squares = pl.pallas_call(
        solve_kernel,
        in_specs=[inside] * 3,
        out_specs=(inside, inside),
        out_shape=(pltpu.VMEM((held, 2 * rank), f32), pltpu.VMEM((SUB, 2 * rank), f32)),
        name="solve",
    )(*held_in(block, other, inverse))
    squares = squares + swap(squares, 0, 0, 1)
    bit = 1
    parts = None
    while bit < neur:
        if bit * 2 < neur:
            parts = [squares] + [swap(squares, k * bit, 0, 1) for k in (1, 2, 3)]
            bit *= 4
        else:
            zero = jnp.zeros_like(squares)
            parts = [squares, swap(squares, bit, 0, 1), zero, zero]
            bit *= 2
        if bit < neur:
            squares = (parts[0] + parts[1]) + (parts[2] + parts[3])
    result, weights = pl.pallas_call(
        functools.partial(scale_kernel, rows * neur),
        in_specs=[inside] * 5,
        out_specs=(inside, inside),
        out_shape=(jax.ShapeDtypeStruct((share, rank), f32), jax.ShapeDtypeStruct((1, rank), f32)),
        name="scale",
    )(*held_in(solved, *parts))
    return (result, weights[0])


def solution(mesh):
    return jax.shard_map(
        functools.partial(local, mesh.shape["neur"], mesh.shape["tri"]),
        mesh=mesh,
        in_specs=(P("neur", "tri", "bin"), P("bin", None), P("tri", None)),
        out_specs=(P(("neur", "tri", "bin"), None), P()),
        check_vma=False,
    )
```

```python
import functools

import jax
import jax.numpy as jnp
from jax import lax
from jax.experimental import pallas as pl
from jax.experimental.pallas import tpu as pltpu
from jax.sharding import PartitionSpec as P

SUB = 8
EXACT = lax.Precision.HIGHEST


def held_in(*values):
    return [pltpu.with_memory_space_constraint(value, pltpu.VMEM) for value in values]


def parity(index, count):
    result = index & 1
    for bit in range(1, count.bit_length() - 1):
        result = result ^ ((index >> bit) & 1)
    return result


def gram_of(factor_t):
    return lax.dot_general(factor_t, factor_t, (((1,), (1,)), ((), ())), preferred_element_type=jnp.float32)


def packed(value):
    count = value.shape[0] // 2
    return jnp.concatenate([value[:count], value[count:]], axis=1)


def product_kernel(
    tri, tensor_ref, bin_t_ref, trial_ref, send_ref, own_ref, gram_ref, block_ref, bin_ref, local_ref, wide_ref, sems
):
    neurons, trials, bins = block_ref.shape
    rank = bin_ref.shape[0]
    pair = trials // 2
    share = neurons // (2 * tri)
    rows = share // 2
    bin_copy = pltpu.make_async_copy(bin_t_ref, bin_ref, sems.at[0])
    trial_copy = pltpu.make_async_copy(trial_ref, local_ref, sems.at[1])
    groups = ((0, 1), (2, 3))
    copies = []
    for i, g in enumerate(groups):
        span = pl.ds(2 * g[0] * share, 2 * len(g) * share)
        copies.append(pltpu.make_async_copy(tensor_ref.at[span], block_ref.at[span], sems.at[2 + i]))
    bin_copy.start()
    trial_copy.start()
    for copy in copies:
        copy.start()
    half = lax.axis_index("bin") ^ parity(lax.axis_index("tri"), tri)
    bin_copy.wait()
    bin_t = bin_ref[...]
    gram = lax.dot_general(bin_t, bin_t, (((1,), (1,)), ((), ())), preferred_element_type=jnp.float32)
    send_ref[rows * tri :, :] = packed(gram)
    factor = bin_t.T
    zero = jnp.zeros_like(factor)
    wide_ref[:bins, :] = jnp.concatenate([factor, zero], axis=1)
    wide_ref[bins:, :] = jnp.concatenate([zero, factor], axis=1)
    trial_copy.wait()
    trial = local_ref[...]
    gram = lax.dot_general(trial, trial, (((0,), (0,)), ((), ())), preferred_element_type=jnp.float32)
    gram_ref[...] = packed(gram)
    trial = packed(trial.astype(jnp.float32))
    left = lax.broadcasted_iota(jnp.int32, (rows, 2 * rank), 1) < rank
    wide = wide_ref[...]
    for i, g in enumerate(groups):
        copies[i].wait()
        for t in g:
            for out_ref, side in ((send_ref, 1), (own_ref, 0)):
                first = (2 * t + (half ^ parity(t, tri) ^ side)) * share
                part = block_ref.at[pl.ds(first, share)]
                low = part[:, :pair, :].reshape(share * pair, bins)
                high = part[:, pair:, :].reshape(share * pair, bins)
                section = jnp.dot(jnp.concatenate([low, high], axis=1), wide, preferred_element_type=jnp.float32)
                total = jnp.sum(section.reshape(share, pair, 2 * rank) * trial[None], axis=1)
                total = total + pltpu.roll(total, rank, 1)
                out_ref[t * rows : (t + 1) * rows, :] = jnp.where(left, total[:rows], total[rows:])


def products(tri, tensor, bin_t, trial_factor):
    neurons, trials, bins = tensor.shape
    rank = bin_t.shape[0]
    rows = neurons // 4
    f32 = jnp.float32
    anywhere = pl.BlockSpec(memory_space=pl.ANY)
    inside = pl.BlockSpec(memory_space=pltpu.VMEM)
    return pl.pallas_call(
        functools.partial(product_kernel, tri),
        in_specs=[anywhere] * 3,
        out_specs=(inside,) * 3,
        out_shape=(
            pltpu.VMEM((rows + rank // 2, 2 * rank), f32),
            pltpu.VMEM((rows, 2 * rank), f32),
            pltpu.VMEM((rank // 2, 2 * rank), f32),
        ),
        scratch_shapes=[
            pltpu.VMEM((neurons, trials, bins), jnp.bfloat16),
            pltpu.VMEM((rank, bins), jnp.bfloat16),
            pltpu.VMEM((trials, rank), jnp.bfloat16),
            pltpu.VMEM((2 * bins, 2 * rank), jnp.bfloat16),
            pltpu.SemaphoreType.DMA((8,)),
        ],
        name="products",
    )(tensor, bin_t, trial_factor)


def inverse_tiles(tiles):
    shape = tiles[0].shape
    count = len(tiles)
    lane = lax.broadcasted_iota(jnp.int32, shape, 1)
    sub = lax.broadcasted_iota(jnp.int32, shape, 0)
    across = lambda tile, j: jnp.broadcast_to(tile[:, j : j + 1], shape)
    down = lambda tile, i: jnp.broadcast_to(tile[i : i + 1, :], shape)
    for panel in range(count):
        base = panel * SUB
        columns = [across(tiles[panel], base + j) for j in range(SUB)]
        block = tiles[panel]
        for k in range(SUB):
            scale = 1.0 / down(columns[k], k)
            column = columns[k]
            row = jnp.where(lane == base + k, 1.0, down(block, k)) * scale
            block = jnp.where(sub == k, row, jnp.where(lane == base + k, 0.0, block) - column * row)
            for j in range(k + 1, SUB):
                row = down(columns[j], k) * scale
                columns[j] = jnp.where(sub == k, row, columns[j] - column * row)
        inside = (lane >= base) & (lane < base + SUB)
        rows = [down(block, j) for j in range(SUB)]
        updated = {panel: block}
        for index in range(1, count):
            index = (panel + index) % count
            tile = tiles[index]
            even = across(tile, base) * rows[0]
            odd = jnp.where(inside, 0.0, tile)
            for j in range(1, SUB):
                if j % 2:
                    odd = odd - across(tile, base + j) * rows[j]
                else:
                    even = even + across(tile, base + j) * rows[j]
            updated[index] = odd - even
        tiles = [updated[index] for index in range(count)]
    return tiles


def inverse_kernel(bin_a_ref, bin_b_ref, trial_a_ref, trial_b_ref, out_ref):
    rank = out_ref.shape[0] // 2
    gram = (bin_a_ref[...] + bin_b_ref[...]) * (trial_a_ref[...] + trial_b_ref[...])
    tiles = [gram[i : i + SUB, lane : lane + rank] for lane in (0, rank) for i in range(0, rank // 2, SUB)]
    zero = jnp.zeros_like(tiles[0])
    for i, tile in enumerate(inverse_tiles(tiles)):
        out_ref[i * SUB : (i + 1) * SUB, :] = jnp.concatenate([tile, zero], axis=1)
        out_ref[rank + i * SUB : rank + (i + 1) * SUB, :] = jnp.concatenate([zero, tile], axis=1)


def solve_kernel(own_ref, other_ref, inverse_ref, solved_ref, squares_ref):
    rank = inverse_ref.shape[0] // 2
    solved = jnp.dot(own_ref[...] + other_ref[...], inverse_ref[...], preferred_element_type=jnp.float32, precision=EXACT)
    solved_ref[...] = solved
    squares = jnp.sum(solved * solved, axis=0, keepdims=True)
    squares = jnp.broadcast_to(squares, squares_ref.shape)
    squares_ref[...] = squares + pltpu.roll(squares, rank, 1)


def scale_kernel(count, solved_ref, one_ref, two_ref, three_ref, four_ref, out_ref, weights_ref):
    share, rank = out_ref.shape
    rows = share // 2
    squares = (one_ref[...] + two_ref[...]) + (three_ref[...] + four_ref[...])
    weights = jnp.sqrt(squares[:1] / count + 1e-06)
    weights_ref[...] = weights[:, :rank]
    mine = solved_ref[pl.ds(pl.multiple_of(lax.axis_index("tri") * rows, SUB), rows), :] / weights
    out_ref[:rows, :] = mine[:, :rank]
    out_ref[rows:, :] = mine[:, rank:]


def local(neur, tri, tensor, bin_factor, trial_factor):
    axes = ("neur", "tri", "bin")
    rank = bin_factor.shape[1]
    f32 = jnp.float32

    def exchange(value, partner):
        flat = lambda n, t, b: (n * tri + t) * 2 + b
        places = [(n, t, b) for n in range(neur) for t in range(tri) for b in range(2)]
        return lax.ppermute(value, axes, [(flat(*place), flat(*partner(*place))) for place in places])

    def swap(value, n, t, b):
        return exchange(value, lambda i, j, k: (i ^ n, j ^ t, k ^ b))

    rows = tensor.shape[0]
    held = rows // 4
    share = rows // (2 * tri)
    sent, own, trial_gram = products(tri, tensor, bin_factor.T, trial_factor)
    got = swap(sent, 0, 0, 1)
    bin_a, bin_b = sent[held:], got[held:]
    block = own + got[:held]
    joined = jnp.concatenate([block, trial_gram], axis=0)
    bit = 1
    while bit < tri // 2:
        joined = joined + swap(joined, 0, bit, 1)
        bit *= 2
    other = swap(joined, 0, bit, 1)
    block, other_block = joined[:held], other[:held]
    trial_gram, trial_other = joined[held:], other[held:]
    inside = pl.BlockSpec(memory_space=pltpu.VMEM)
    inverse = pl.pallas_call(
        inverse_kernel,
        in_specs=[inside] * 4,
        out_specs=inside,
        out_shape=pltpu.VMEM((2 * rank, 2 * rank), f32),
        name="inverse",
    )(*held_in(bin_a, bin_b, trial_gram, trial_other))
    solved, squares = pl.pallas_call(
        solve_kernel,
        in_specs=[inside] * 3,
        out_specs=(inside, inside),
        out_shape=(pltpu.VMEM((held, 2 * rank), f32), pltpu.VMEM((SUB, 2 * rank), f32)),
        name="solve",
    )(*held_in(block, other_block, inverse))
    squares = squares + swap(squares, 0, 0, 1)
    bit = 1
    parts = None
    while bit < neur:
        if bit * 2 < neur:
            far = exchange(squares, lambda n, t, b: (n ^ ((2 + b) * bit), t, b))
            near = swap(squares, bit, 0, 1)
            parts = [squares, near, far, swap(far, 0, 0, 1)]
            bit *= 4
        else:
            zero = jnp.zeros_like(squares)
            parts = [squares, swap(squares, bit, 0, 1), zero, zero]
            bit *= 2
        if bit < neur:
            squares = (parts[0] + parts[1]) + (parts[2] + parts[3])
    result, weights = pl.pallas_call(
        functools.partial(scale_kernel, rows * neur),
        in_specs=[inside] * 5,
        out_specs=(inside, inside),
        out_shape=(jax.ShapeDtypeStruct((share, rank), f32), jax.ShapeDtypeStruct((1, rank), f32)),
        name="scale",
    )(*held_in(solved, *parts))
    return (result, weights[0])


def solution(mesh):
    return jax.shard_map(
        functools.partial(local, mesh.shape["neur"], mesh.shape["tri"]),
        mesh=mesh,
        in_specs=(P("neur", "tri", "bin"), P("bin", None), P("tri", None)),
        out_specs=(P(("neur", "tri", "bin"), None), P()),
        check_vma=False,
    )
```

```python
import functools

import jax
import jax.numpy as jnp
from jax import lax
from jax.experimental import pallas as pl
from jax.experimental.pallas import tpu as pltpu
from jax.sharding import PartitionSpec as P

SUB = 8
GRANT = 16 * 2**20
EXACT = lax.Precision.HIGHEST


def held_in(*values):
    return [pltpu.with_memory_space_constraint(value, pltpu.VMEM) for value in values]


def parity(index, count):
    result = index & 1
    for bit in range(1, count.bit_length() - 1):
        result = result ^ ((index >> bit) & 1)
    return result


def gram_of(factor_t):
    return lax.dot_general(factor_t, factor_t, (((1,), (1,)), ((), ())), preferred_element_type=jnp.float32)


def packed(value):
    count = value.shape[0] // 2
    return jnp.concatenate([value[:count], value[count:]], axis=1)


def row_products(part, wide, trial, left):
    share, trials, bins = part.shape
    pair = trials // 2
    rank = wide.shape[1] // 2
    rows = share // 2
    low = part[:, :pair, :].reshape(share * pair, bins)
    high = part[:, pair:, :].reshape(share * pair, bins)
    section = jnp.dot(jnp.concatenate([low, high], axis=1), wide, preferred_element_type=jnp.float32)
    total = jnp.sum(section.reshape(share, pair, 2 * rank) * trial[None], axis=1)
    total = total + pltpu.roll(total, rank, 1)
    return jnp.where(left, total[:rows], total[rows:])


def send_kernel(tri, tensor_ref, bin_t_ref, trial_ref, send_ref, gram_ref, held_ref, local_ref, wide_ref, block_ref, bin_ref, sems):
    neurons, trials, bins = tensor_ref.shape
    rank = bin_ref.shape[0]
    share = neurons // (2 * tri)
    rows = share // 2
    half = lax.axis_index("bin") ^ parity(lax.axis_index("tri"), tri)
    bin_copy = pltpu.make_async_copy(bin_t_ref, bin_ref, sems.at[0])
    trial_copy = pltpu.make_async_copy(trial_ref, local_ref, sems.at[1])
    bin_copy.start()
    trial_copy.start()
    copies = []
    for side, target in ((1, block_ref), (0, held_ref)):
        for t in range(tri):
            first = (2 * t + (half ^ parity(t, tri) ^ side)) * share
            copy = pltpu.make_async_copy(
                tensor_ref.at[pl.ds(first, share)], target.at[pl.ds(t * share, share)], sems.at[2 + len(copies)]
            )
            copy.start()
            copies.append(copy)
    bin_copy.wait()
    bin_t = bin_ref[...]
    gram = lax.dot_general(bin_t, bin_t, (((1,), (1,)), ((), ())), preferred_element_type=jnp.float32)
    send_ref[rows * tri :, :] = packed(gram)
    factor = bin_t.T
    zero = jnp.zeros_like(factor)
    wide_ref[:bins, :] = jnp.concatenate([factor, zero], axis=1)
    wide_ref[bins:, :] = jnp.concatenate([zero, factor], axis=1)
    trial_copy.wait()
    local = local_ref[...]
    gram = lax.dot_general(local, local, (((0,), (0,)), ((), ())), preferred_element_type=jnp.float32)
    gram_ref[...] = packed(gram)
    trial = packed(local.astype(jnp.float32))
    left = lax.broadcasted_iota(jnp.int32, (rows, 2 * rank), 1) < rank
    wide = wide_ref[...]
    for copy in copies[:tri]:
        copy.wait()
    for t in range(tri):
        send_ref[t * rows : (t + 1) * rows, :] = row_products(block_ref.at[pl.ds(t * share, share)], wide, trial, left)
    for copy in copies[tri:]:
        copy.wait()


def own_kernel(tri, held_ref, local_ref, wide_ref, own_ref):
    share = held_ref.shape[0] // tri
    rows = share // 2
    rank = local_ref.shape[1]
    local = local_ref[...]
    trial = packed(local.astype(jnp.float32))
    left = lax.broadcasted_iota(jnp.int32, (rows, 2 * rank), 1) < rank
    wide = wide_ref[...]
    for t in range(tri):
        own_ref[t * rows : (t + 1) * rows, :] = row_products(held_ref.at[pl.ds(t * share, share)], wide, trial, left)


def send_products(tri, tensor, bin_t, trial_factor):
    neurons, trials, bins = tensor.shape
    rank = bin_t.shape[0]
    outside = pl.BlockSpec(memory_space=pltpu.HBM)
    inside = pl.BlockSpec(memory_space=pltpu.VMEM)
    return pl.pallas_call(
        functools.partial(send_kernel, tri),
        in_specs=[outside] * 3,
        out_specs=(inside,) * 5,
        out_shape=(
            pltpu.VMEM((neurons // 4 + rank // 2, 2 * rank), jnp.float32),
            pltpu.VMEM((rank // 2, 2 * rank), jnp.float32),
            pltpu.VMEM((neurons // 2, trials, bins), jnp.bfloat16),
            pltpu.VMEM((trials, rank), jnp.bfloat16),
            pltpu.VMEM((2 * bins, 2 * rank), jnp.bfloat16),
        ),
        scratch_shapes=[
            pltpu.VMEM((neurons // 2, trials, bins), jnp.bfloat16),
            pltpu.VMEM((rank, bins), jnp.bfloat16),
            pltpu.SemaphoreType.DMA((2 + 2 * tri,)),
        ],
        compiler_params=pltpu.CompilerParams(vmem_limit_bytes=GRANT),
        name="send_products",
    )(*(pltpu.with_memory_space_constraint(value, pltpu.HBM) for value in (tensor, bin_t, trial_factor)))


def own_products(tri, held, local, wide):
    rank = local.shape[1]
    inside = pl.BlockSpec(memory_space=pltpu.VMEM)
    return pl.pallas_call(
        functools.partial(own_kernel, tri),
        in_specs=[inside] * 3,
        out_specs=inside,
        out_shape=pltpu.VMEM((held.shape[0] // 2, 2 * rank), jnp.float32),
        compiler_params=pltpu.CompilerParams(vmem_limit_bytes=GRANT),
        name="own_products",
    )(*held_in(held, local, wide))


def inverse_tiles(tiles):
    shape = tiles[0].shape
    count = len(tiles)
    lane = lax.broadcasted_iota(jnp.int32, shape, 1)
    sub = lax.broadcasted_iota(jnp.int32, shape, 0)
    across = lambda tile, j: jnp.broadcast_to(tile[:, j : j + 1], shape)
    down = lambda tile, i: jnp.broadcast_to(tile[i : i + 1, :], shape)
    for panel in range(count):
        base = panel * SUB
        columns = [across(tiles[panel], base + j) for j in range(SUB)]
        block = tiles[panel]
        for k in range(SUB):
            scale = 1.0 / down(columns[k], k)
            column = columns[k]
            row = jnp.where(lane == base + k, 1.0, down(block, k)) * scale
            block = jnp.where(sub == k, row, jnp.where(lane == base + k, 0.0, block) - column * row)
            for j in range(k + 1, SUB):
                row = down(columns[j], k) * scale
                columns[j] = jnp.where(sub == k, row, columns[j] - column * row)
        inside = (lane >= base) & (lane < base + SUB)
        rows = [down(block, j) for j in range(SUB)]
        updated = {panel: block}
        for index in range(1, count):
            index = (panel + index) % count
            tile = tiles[index]
            even = across(tile, base) * rows[0]
            odd = jnp.where(inside, 0.0, tile)
            for j in range(1, SUB):
                if j % 2:
                    odd = odd - across(tile, base + j) * rows[j]
                else:
                    even = even + across(tile, base + j) * rows[j]
            updated[index] = odd - even
        tiles = [updated[index] for index in range(count)]
    return tiles


def add_kernel(one_ref, two_ref, out_ref):
    out_ref[...] = one_ref[...] + two_ref[...]


def added(one, two):
    inside = pl.BlockSpec(memory_space=pltpu.VMEM)
    return pl.pallas_call(
        add_kernel,
        in_specs=[inside] * 2,
        out_specs=inside,
        out_shape=pltpu.VMEM(one.shape, one.dtype),
        cost_estimate=pl.CostEstimate(flops=10000000000, bytes_accessed=200000, transcendentals=0),
        name="added",
    )(*held_in(one, two))


def inverse_kernel(bin_a_ref, bin_b_ref, trial_a_ref, trial_b_ref, out_ref):
    rank = out_ref.shape[0] // 2
    gram = (bin_a_ref[...] + bin_b_ref[...]) * (trial_a_ref[...] + trial_b_ref[...])
    tiles = [gram[i : i + SUB, lane : lane + rank] for lane in (0, rank) for i in range(0, rank // 2, SUB)]
    zero = jnp.zeros_like(tiles[0])
    for i, tile in enumerate(inverse_tiles(tiles)):
        out_ref[i * SUB : (i + 1) * SUB, :] = jnp.concatenate([tile, zero], axis=1)
        out_ref[rank + i * SUB : rank + (i + 1) * SUB, :] = jnp.concatenate([zero, tile], axis=1)


def solve_kernel(own_ref, other_ref, inverse_ref, solved_ref, squares_ref):
    rank = inverse_ref.shape[0] // 2
    solved = jnp.dot(own_ref[...] + other_ref[...], inverse_ref[...], preferred_element_type=jnp.float32, precision=EXACT)
    solved_ref[...] = solved
    squares = jnp.sum(solved * solved, axis=0, keepdims=True)
    squares = jnp.broadcast_to(squares, squares_ref.shape)
    squares_ref[...] = squares + pltpu.roll(squares, rank, 1)


def scale_kernel(count, solved_ref, one_ref, two_ref, three_ref, four_ref, out_ref, weights_ref):
    share, rank = out_ref.shape
    rows = share // 2
    squares = (one_ref[...] + two_ref[...]) + (three_ref[...] + four_ref[...])
    weights = jnp.sqrt(squares[:1] / count + 1e-06)
    weights_ref[...] = weights[:, :rank]
    mine = solved_ref[pl.ds(pl.multiple_of(lax.axis_index("tri") * rows, SUB), rows), :] / weights
    out_ref[:rows, :] = mine[:, :rank]
    out_ref[rows:, :] = mine[:, rank:]


def local(neur, tri, tensor, bin_factor, trial_factor):
    axes = ("neur", "tri", "bin")
    rank = bin_factor.shape[1]
    f32 = jnp.float32

    def exchange(value, partner):
        flat = lambda n, t, b: (n * tri + t) * 2 + b
        places = [(n, t, b) for n in range(neur) for t in range(tri) for b in range(2)]
        return lax.ppermute(value, axes, [(flat(*place), flat(*partner(*place))) for place in places])

    def swap(value, n, t, b):
        return exchange(value, lambda i, j, k: (i ^ n, j ^ t, k ^ b))

    rows = tensor.shape[0]
    held = rows // 4
    share = rows // (2 * tri)
    sent, trial_gram, kept, local_factor, wide = send_products(tri, tensor, bin_factor.T, trial_factor)
    got = swap(sent, 0, 0, 1)
    own = own_products(tri, kept, local_factor, wide)
    bin_a, bin_b = sent[held:], got[held:]
    block = own + got[:held]
    bit = 1
    while bit < tri // 2:
        trial_gram = added(trial_gram, swap(trial_gram, 0, bit, 1))
        block = block + swap(block, 0, bit, 1)
        bit *= 2
    trial_other = swap(trial_gram, 0, bit, 1)
    other_block = swap(block, 0, bit, 1)
    inside = pl.BlockSpec(memory_space=pltpu.VMEM)
    inverse = pl.pallas_call(
        inverse_kernel,
        in_specs=[inside] * 4,
        out_specs=inside,
        out_shape=pltpu.VMEM((2 * rank, 2 * rank), f32),
        cost_estimate=pl.CostEstimate(flops=10000000000, bytes_accessed=200000, transcendentals=0),
        name="inverse",
    )(*held_in(bin_a, bin_b, trial_gram, trial_other))
    solved, squares = pl.pallas_call(
        solve_kernel,
        in_specs=[inside] * 3,
        out_specs=(inside, inside),
        out_shape=(pltpu.VMEM((held, 2 * rank), f32), pltpu.VMEM((SUB, 2 * rank), f32)),
        name="solve",
    )(*held_in(block, other_block, inverse))
    squares = squares + swap(squares, 0, 0, 1)
    bit = 1
    parts = None
    while bit < neur:
        if bit * 2 < neur:
            far = exchange(squares, lambda n, t, b: (n ^ ((2 + b) * bit), t, b))
            near = swap(squares, bit, 0, 1)
            parts = [squares, near, far, swap(far, 0, 0, 1)]
            bit *= 4
        else:
            zero = jnp.zeros_like(squares)
            parts = [squares, swap(squares, bit, 0, 1), zero, zero]
            bit *= 2
        if bit < neur:
            squares = (parts[0] + parts[1]) + (parts[2] + parts[3])
    result, weights = pl.pallas_call(
        functools.partial(scale_kernel, rows * neur),
        in_specs=[inside] * 5,
        out_specs=(inside, inside),
        out_shape=(jax.ShapeDtypeStruct((share, rank), f32), jax.ShapeDtypeStruct((1, rank), f32)),
        name="scale",
    )(*held_in(solved, *parts))
    return (result, weights[0])


def solution(mesh):
    return jax.shard_map(
        functools.partial(local, mesh.shape["neur"], mesh.shape["tri"]),
        mesh=mesh,
        in_specs=(P("neur", "tri", "bin"), P("bin", None), P("tri", None)),
        out_specs=(P(("neur", "tri", "bin"), None), P()),
        check_vma=False,
    )
```

```python
import functools

import jax
import jax.numpy as jnp
from jax import lax
from jax.experimental import pallas as pl
from jax.experimental.pallas import tpu as pltpu
from jax.sharding import PartitionSpec as P

SUB = 8
GRANT = 16 * 2**20
EXACT = lax.Precision.HIGHEST


def held_in(*values):
    return [pltpu.with_memory_space_constraint(value, pltpu.VMEM) for value in values]


def parity(index, count):
    result = index & 1
    for bit in range(1, count.bit_length() - 1):
        result = result ^ ((index >> bit) & 1)
    return result


def gram_of(factor_t):
    return lax.dot_general(factor_t, factor_t, (((1,), (1,)), ((), ())), preferred_element_type=jnp.float32)


def packed(value):
    count = value.shape[0] // 2
    return jnp.concatenate([value[:count], value[count:]], axis=1)


def row_products(part, wide, trial, left):
    share, trials, bins = part.shape
    pair = trials // 2
    rank = wide.shape[1] // 2
    rows = share // 2
    low = part[:, :pair, :].reshape(share * pair, bins)
    high = part[:, pair:, :].reshape(share * pair, bins)
    section = jnp.dot(jnp.concatenate([low, high], axis=1), wide, preferred_element_type=jnp.float32)
    total = jnp.sum(section.reshape(share, pair, 2 * rank) * trial[None], axis=1)
    total = total + pltpu.roll(total, rank, 1)
    return jnp.where(left, total[:rows], total[rows:])


def send_kernel(tri, tensor_ref, bin_t_ref, trial_ref, send_ref, gram_ref, held_ref, local_ref, wide_ref, block_ref, bin_ref, sems):
    neurons, trials, bins = tensor_ref.shape
    rank = bin_ref.shape[0]
    share = neurons // (2 * tri)
    rows = share // 2
    half = lax.axis_index("bin") ^ parity(lax.axis_index("tri"), tri)
    bin_copy = pltpu.make_async_copy(bin_t_ref, bin_ref, sems.at[0])
    trial_copy = pltpu.make_async_copy(trial_ref, local_ref, sems.at[1])
    bin_copy.start()
    trial_copy.start()
    copies = []
    for side, target in ((1, block_ref), (0, held_ref)):
        for t in range(tri):
            first = (2 * t + (half ^ parity(t, tri) ^ side)) * share
            copy = pltpu.make_async_copy(
                tensor_ref.at[pl.ds(first, share)], target.at[pl.ds(t * share, share)], sems.at[2 + len(copies)]
            )
            copy.start()
            copies.append(copy)
    bin_copy.wait()
    bin_t = bin_ref[...]
    gram = lax.dot_general(bin_t, bin_t, (((1,), (1,)), ((), ())), preferred_element_type=jnp.float32)
    send_ref[rows * tri :, :] = packed(gram)
    factor = bin_t.T
    zero = jnp.zeros_like(factor)
    wide_ref[:bins, :] = jnp.concatenate([factor, zero], axis=1)
    wide_ref[bins:, :] = jnp.concatenate([zero, factor], axis=1)
    trial_copy.wait()
    local = local_ref[...]
    gram = lax.dot_general(local, local, (((0,), (0,)), ((), ())), preferred_element_type=jnp.float32)
    gram_ref[...] = packed(gram)
    trial = packed(local.astype(jnp.float32))
    left = lax.broadcasted_iota(jnp.int32, (rows, 2 * rank), 1) < rank
    wide = wide_ref[...]
    for t in range(tri):
        if t % 2 == 0:
            for copy in copies[t : min(t + 2, tri)]:
                copy.wait()
        send_ref[t * rows : (t + 1) * rows, :] = row_products(block_ref.at[pl.ds(t * share, share)], wide, trial, left)
    for copy in copies[tri:]:
        copy.wait()


def own_kernel(tri, held_ref, local_ref, wide_ref, own_ref):
    share = held_ref.shape[0] // tri
    rows = share // 2
    rank = local_ref.shape[1]
    local = local_ref[...]
    trial = packed(local.astype(jnp.float32))
    left = lax.broadcasted_iota(jnp.int32, (rows, 2 * rank), 1) < rank
    wide = wide_ref[...]
    for t in range(tri):
        own_ref[t * rows : (t + 1) * rows, :] = row_products(held_ref.at[pl.ds(t * share, share)], wide, trial, left)


def send_products(tri, tensor, bin_t, trial_factor):
    neurons, trials, bins = tensor.shape
    rank = bin_t.shape[0]
    outside = pl.BlockSpec(memory_space=pltpu.HBM)
    inside = pl.BlockSpec(memory_space=pltpu.VMEM)
    return pl.pallas_call(
        functools.partial(send_kernel, tri),
        in_specs=[outside] * 3,
        out_specs=(inside,) * 5,
        out_shape=(
            pltpu.VMEM((neurons // 4 + rank // 2, 2 * rank), jnp.float32),
            pltpu.VMEM((rank // 2, 2 * rank), jnp.float32),
            pltpu.VMEM((neurons // 2, trials, bins), jnp.bfloat16),
            pltpu.VMEM((trials, rank), jnp.bfloat16),
            pltpu.VMEM((2 * bins, 2 * rank), jnp.bfloat16),
        ),
        scratch_shapes=[
            pltpu.VMEM((neurons // 2, trials, bins), jnp.bfloat16),
            pltpu.VMEM((rank, bins), jnp.bfloat16),
            pltpu.SemaphoreType.DMA((2 + 2 * tri,)),
        ],
        compiler_params=pltpu.CompilerParams(vmem_limit_bytes=GRANT),
        name="send_products",
    )(*(pltpu.with_memory_space_constraint(value, pltpu.HBM) for value in (tensor, bin_t, trial_factor)))


def own_products(tri, held, local, wide):
    rank = local.shape[1]
    inside = pl.BlockSpec(memory_space=pltpu.VMEM)
    return pl.pallas_call(
        functools.partial(own_kernel, tri),
        in_specs=[inside] * 3,
        out_specs=inside,
        out_shape=pltpu.VMEM((held.shape[0] // 2, 2 * rank), jnp.float32),
        compiler_params=pltpu.CompilerParams(vmem_limit_bytes=GRANT),
        name="own_products",
    )(*held_in(held, local, wide))


def inverse_tiles(tiles):
    shape = tiles[0].shape
    count = len(tiles)
    lane = lax.broadcasted_iota(jnp.int32, shape, 1)
    sub = lax.broadcasted_iota(jnp.int32, shape, 0)
    across = lambda tile, j: jnp.broadcast_to(tile[:, j : j + 1], shape)
    down = lambda tile, i: jnp.broadcast_to(tile[i : i + 1, :], shape)
    for panel in range(count):
        base = panel * SUB
        columns = [across(tiles[panel], base + j) for j in range(SUB)]
        block = tiles[panel]
        for k in range(SUB):
            scale = 1.0 / down(columns[k], k)
            column = columns[k]
            row = jnp.where(lane == base + k, 1.0, down(block, k)) * scale
            block = jnp.where(sub == k, row, jnp.where(lane == base + k, 0.0, block) - column * row)
            for j in range(k + 1, SUB):
                row = down(columns[j], k) * scale
                columns[j] = jnp.where(sub == k, row, columns[j] - column * row)
        inside = (lane >= base) & (lane < base + SUB)
        rows = [down(block, j) for j in range(SUB)]
        updated = {panel: block}
        for index in range(1, count):
            index = (panel + index) % count
            tile = tiles[index]
            even = across(tile, base) * rows[0]
            odd = jnp.where(inside, 0.0, tile)
            for j in range(1, SUB):
                if j % 2:
                    odd = odd - across(tile, base + j) * rows[j]
                else:
                    even = even + across(tile, base + j) * rows[j]
            updated[index] = odd - even
        tiles = [updated[index] for index in range(count)]
    return tiles


def add_kernel(one_ref, two_ref, out_ref):
    out_ref[...] = one_ref[...] + two_ref[...]


def added(one, two):
    inside = pl.BlockSpec(memory_space=pltpu.VMEM)
    return pl.pallas_call(
        add_kernel,
        in_specs=[inside] * 2,
        out_specs=inside,
        out_shape=pltpu.VMEM(one.shape, one.dtype),
        cost_estimate=pl.CostEstimate(flops=10000000000, bytes_accessed=200000, transcendentals=0),
        name="added",
    )(*held_in(one, two))


def inverse_kernel(bin_a_ref, bin_b_ref, trial_a_ref, trial_b_ref, out_ref):
    rank = out_ref.shape[0] // 2
    gram = (bin_a_ref[...] + bin_b_ref[...]) * (trial_a_ref[...] + trial_b_ref[...])
    tiles = [gram[i : i + SUB, lane : lane + rank] for lane in (0, rank) for i in range(0, rank // 2, SUB)]
    zero = jnp.zeros_like(tiles[0])
    for i, tile in enumerate(inverse_tiles(tiles)):
        out_ref[i * SUB : (i + 1) * SUB, :] = jnp.concatenate([tile, zero], axis=1)
        out_ref[rank + i * SUB : rank + (i + 1) * SUB, :] = jnp.concatenate([zero, tile], axis=1)


def solve_kernel(own_ref, other_ref, inverse_ref, solved_ref, squares_ref):
    rank = inverse_ref.shape[0] // 2
    solved = jnp.dot(own_ref[...] + other_ref[...], inverse_ref[...], preferred_element_type=jnp.float32, precision=EXACT)
    solved_ref[...] = solved
    squares = jnp.sum(solved * solved, axis=0, keepdims=True)
    squares = jnp.broadcast_to(squares, squares_ref.shape)
    squares_ref[...] = squares + pltpu.roll(squares, rank, 1)


def scale_kernel(count, solved_ref, one_ref, two_ref, three_ref, four_ref, out_ref, weights_ref):
    share, rank = out_ref.shape
    rows = share // 2
    squares = (one_ref[...] + two_ref[...]) + (three_ref[...] + four_ref[...])
    weights = jnp.sqrt(squares[:1] / count + 1e-06)
    weights_ref[...] = weights[:, :rank]
    mine = solved_ref[pl.ds(pl.multiple_of(lax.axis_index("tri") * rows, SUB), rows), :] / weights
    out_ref[:rows, :] = mine[:, :rank]
    out_ref[rows:, :] = mine[:, rank:]


def local(neur, tri, tensor, bin_factor, trial_factor):
    axes = ("neur", "tri", "bin")
    rank = bin_factor.shape[1]
    f32 = jnp.float32

    def exchange(value, partner):
        flat = lambda n, t, b: (n * tri + t) * 2 + b
        places = [(n, t, b) for n in range(neur) for t in range(tri) for b in range(2)]
        return lax.ppermute(value, axes, [(flat(*place), flat(*partner(*place))) for place in places])

    def swap(value, n, t, b):
        return exchange(value, lambda i, j, k: (i ^ n, j ^ t, k ^ b))

    rows = tensor.shape[0]
    held = rows // 4
    share = rows // (2 * tri)
    sent, trial_gram, kept, local_factor, wide = send_products(tri, tensor, bin_factor.T, trial_factor)
    got = swap(sent, 0, 0, 1)
    own = own_products(tri, kept, local_factor, wide)
    bin_a, bin_b = sent[held:], got[held:]
    stages = tri.bit_length() - 1

    def cross(value, stage):
        return exchange(value, lambda n, t, b: (n, t ^ (1 << (stage + (b ^ parity(t, tri))) % stages), 1 - b))

    block = own + got[:held]
    for stage in range(stages - 1):
        trial_gram = added(trial_gram, cross(trial_gram, stage))
        block = block + cross(block, stage)
    trial_other = cross(trial_gram, stages - 1)
    other_block = cross(block, stages - 1)
    inside = pl.BlockSpec(memory_space=pltpu.VMEM)
    inverse = pl.pallas_call(
        inverse_kernel,
        in_specs=[inside] * 4,
        out_specs=inside,
        out_shape=pltpu.VMEM((2 * rank, 2 * rank), f32),
        cost_estimate=pl.CostEstimate(flops=10000000000, bytes_accessed=200000, transcendentals=0),
        name="inverse",
    )(*held_in(bin_a, bin_b, trial_gram, trial_other))
    solved, squares = pl.pallas_call(
        solve_kernel,
        in_specs=[inside] * 3,
        out_specs=(inside, inside),
        out_shape=(pltpu.VMEM((held, 2 * rank), f32), pltpu.VMEM((SUB, 2 * rank), f32)),
        name="solve",
    )(*held_in(block, other_block, inverse))
    squares = squares + swap(squares, 0, 0, 1)
    bit = 1
    parts = None
    while bit < neur:
        if bit * 2 < neur:
            far = exchange(squares, lambda n, t, b: (n ^ ((2 + b) * bit), t, b))
            near = swap(squares, bit, 0, 1)
            parts = [squares, near, far, swap(far, 0, 0, 1)]
            bit *= 4
        else:
            zero = jnp.zeros_like(squares)
            parts = [squares, swap(squares, bit, 0, 1), zero, zero]
            bit *= 2
        if bit < neur:
            squares = (parts[0] + parts[1]) + (parts[2] + parts[3])
    result, weights = pl.pallas_call(
        functools.partial(scale_kernel, rows * neur),
        in_specs=[inside] * 5,
        out_specs=(inside, inside),
        out_shape=(jax.ShapeDtypeStruct((share, rank), f32), jax.ShapeDtypeStruct((1, rank), f32)),
        name="scale",
    )(*held_in(solved, *parts))
    return (result, weights[0])


def solution(mesh):
    return jax.shard_map(
        functools.partial(local, mesh.shape["neur"], mesh.shape["tri"]),
        mesh=mesh,
        in_specs=(P("neur", "tri", "bin"), P("bin", None), P("tri", None)),
        out_specs=(P(("neur", "tri", "bin"), None), P()),
        check_vma=False,
    )
```

```python
import functools

import jax
import jax.numpy as jnp
from jax import lax
from jax.experimental import pallas as pl
from jax.experimental.pallas import tpu as pltpu
from jax.sharding import PartitionSpec as P

SUB = 8
GRANT = 16 * 2**20
EXACT = lax.Precision.HIGHEST


def held_in(*values):
    return [pltpu.with_memory_space_constraint(value, pltpu.VMEM) for value in values]


def parity(index, count):
    result = index & 1
    for bit in range(1, count.bit_length() - 1):
        result = result ^ ((index >> bit) & 1)
    return result


def gram_of(factor_t):
    return lax.dot_general(factor_t, factor_t, (((1,), (1,)), ((), ())), preferred_element_type=jnp.float32)


def packed(value):
    count = value.shape[0] // 2
    return jnp.concatenate([value[:count], value[count:]], axis=1)


def sections(part, wide):
    share, trials, bins = part.shape
    pair = trials // 2
    low = part[:, :pair, :].reshape(share * pair, bins)
    high = part[:, pair:, :].reshape(share * pair, bins)
    section = jnp.dot(jnp.concatenate([low, high], axis=1), wide, preferred_element_type=jnp.float32)
    return section.reshape(share, pair, wide.shape[1])


def over_trials(section, trial, left):
    rows = section.shape[0] // 2
    total = jnp.sum(section * trial[None], axis=1)
    total = total + pltpu.roll(total, trial.shape[1] // 2, 1)
    return jnp.where(left, total[:rows], total[rows:])


def row_products(part, wide, trial, left):
    return over_trials(sections(part, wide), trial, left)


def send_kernel(tri, tensor_ref, bin_t_ref, trial_ref, send_ref, gram_ref, held_ref, local_ref, wide_ref, block_ref, bin_ref, sems):
    neurons, trials, bins = tensor_ref.shape
    rank = bin_ref.shape[0]
    share = neurons // (2 * tri)
    rows = share // 2
    half = lax.axis_index("bin") ^ parity(lax.axis_index("tri"), tri)
    bin_copy = pltpu.make_async_copy(bin_t_ref, bin_ref, sems.at[0])
    trial_copy = pltpu.make_async_copy(trial_ref, local_ref, sems.at[1])
    bin_copy.start()
    trial_copy.start()
    copies = []
    for side, target in ((1, block_ref), (0, held_ref)):
        for t in range(tri):
            first = (2 * t + (half ^ parity(t, tri) ^ side)) * share
            copy = pltpu.make_async_copy(
                tensor_ref.at[pl.ds(first, share)], target.at[pl.ds(t * share, share)], sems.at[2 + len(copies)]
            )
            copy.start()
            copies.append(copy)
    bin_copy.wait()
    bin_t = bin_ref[...]
    gram = lax.dot_general(bin_t, bin_t, (((1,), (1,)), ((), ())), preferred_element_type=jnp.float32)
    send_ref[rows * tri :, :] = packed(gram)
    factor = bin_t.T
    zero = jnp.zeros_like(factor)
    wide_ref[:bins, :] = jnp.concatenate([factor, zero], axis=1)
    wide_ref[bins:, :] = jnp.concatenate([zero, factor], axis=1)
    trial_copy.wait()
    local = local_ref[...]
    gram = lax.dot_general(local, local, (((0,), (0,)), ((), ())), preferred_element_type=jnp.float32)
    gram_ref[...] = packed(gram)
    trial = packed(local.astype(jnp.float32))
    left = lax.broadcasted_iota(jnp.int32, (rows, 2 * rank), 1) < rank
    wide = wide_ref[...]
    for copy in copies[: tri // 2]:
        copy.wait()
    early = [sections(block_ref.at[pl.ds(t * share, share)], wide) for t in range(tri // 2)]
    for copy in copies[tri // 2 : tri]:
        copy.wait()
    late = [sections(block_ref.at[pl.ds(t * share, share)], wide) for t in range(tri // 2, tri)]
    for t, section in enumerate(early + late):
        send_ref[t * rows : (t + 1) * rows, :] = over_trials(section, trial, left)
    for copy in copies[tri:]:
        copy.wait()


def own_kernel(tri, held_ref, local_ref, wide_ref, own_ref):
    share = held_ref.shape[0] // tri
    rows = share // 2
    rank = local_ref.shape[1]
    local = local_ref[...]
    trial = packed(local.astype(jnp.float32))
    left = lax.broadcasted_iota(jnp.int32, (rows, 2 * rank), 1) < rank
    wide = wide_ref[...]
    for t in range(tri):
        own_ref[t * rows : (t + 1) * rows, :] = row_products(held_ref.at[pl.ds(t * share, share)], wide, trial, left)


def send_products(tri, tensor, bin_t, trial_factor):
    neurons, trials, bins = tensor.shape
    rank = bin_t.shape[0]
    outside = pl.BlockSpec(memory_space=pltpu.HBM)
    inside = pl.BlockSpec(memory_space=pltpu.VMEM)
    return pl.pallas_call(
        functools.partial(send_kernel, tri),
        in_specs=[outside] * 3,
        out_specs=(inside,) * 5,
        out_shape=(
            pltpu.VMEM((neurons // 4 + rank // 2, 2 * rank), jnp.float32),
            pltpu.VMEM((rank // 2, 2 * rank), jnp.float32),
            pltpu.VMEM((neurons // 2, trials, bins), jnp.bfloat16),
            pltpu.VMEM((trials, rank), jnp.bfloat16),
            pltpu.VMEM((2 * bins, 2 * rank), jnp.bfloat16),
        ),
        scratch_shapes=[
            pltpu.VMEM((neurons // 2, trials, bins), jnp.bfloat16),
            pltpu.VMEM((rank, bins), jnp.bfloat16),
            pltpu.SemaphoreType.DMA((2 + 2 * tri,)),
        ],
        compiler_params=pltpu.CompilerParams(vmem_limit_bytes=GRANT),
        name="send_products",
    )(*(pltpu.with_memory_space_constraint(value, pltpu.HBM) for value in (tensor, bin_t, trial_factor)))


def own_products(tri, held, local, wide):
    rank = local.shape[1]
    inside = pl.BlockSpec(memory_space=pltpu.VMEM)
    return pl.pallas_call(
        functools.partial(own_kernel, tri),
        in_specs=[inside] * 3,
        out_specs=inside,
        out_shape=pltpu.VMEM((held.shape[0] // 2, 2 * rank), jnp.float32),
        compiler_params=pltpu.CompilerParams(vmem_limit_bytes=GRANT),
        name="own_products",
    )(*held_in(held, local, wide))


def inverse_tiles(tiles):
    shape = tiles[0].shape
    count = len(tiles)
    lane = lax.broadcasted_iota(jnp.int32, shape, 1)
    sub = lax.broadcasted_iota(jnp.int32, shape, 0)
    across = lambda tile, j: jnp.broadcast_to(tile[:, j : j + 1], shape)
    down = lambda tile, i: jnp.broadcast_to(tile[i : i + 1, :], shape)
    for panel in range(count):
        base = panel * SUB
        columns = [across(tiles[panel], base + j) for j in range(SUB)]
        block = tiles[panel]
        for k in range(SUB):
            scale = 1.0 / down(columns[k], k)
            column = columns[k]
            row = jnp.where(lane == base + k, 1.0, down(block, k)) * scale
            block = jnp.where(sub == k, row, jnp.where(lane == base + k, 0.0, block) - column * row)
            for j in range(k + 1, SUB):
                row = down(columns[j], k) * scale
                columns[j] = jnp.where(sub == k, row, columns[j] - column * row)
        inside = (lane >= base) & (lane < base + SUB)
        rows = [down(block, j) for j in range(SUB)]
        updated = {panel: block}
        for index in range(1, count):
            index = (panel + index) % count
            tile = tiles[index]
            even = across(tile, base) * rows[0]
            odd = jnp.where(inside, 0.0, tile)
            for j in range(1, SUB):
                if j % 2:
                    odd = odd - across(tile, base + j) * rows[j]
                else:
                    even = even + across(tile, base + j) * rows[j]
            updated[index] = odd - even
        tiles = [updated[index] for index in range(count)]
    return tiles


def add_kernel(one_ref, two_ref, out_ref):
    out_ref[...] = one_ref[...] + two_ref[...]


def added(one, two):
    inside = pl.BlockSpec(memory_space=pltpu.VMEM)
    return pl.pallas_call(
        add_kernel,
        in_specs=[inside] * 2,
        out_specs=inside,
        out_shape=pltpu.VMEM(one.shape, one.dtype),
        cost_estimate=pl.CostEstimate(flops=10000000000, bytes_accessed=200000, transcendentals=0),
        name="added",
    )(*held_in(one, two))


def inverse_kernel(bin_a_ref, bin_b_ref, trial_a_ref, trial_b_ref, out_ref):
    rank = out_ref.shape[0] // 2
    gram = (bin_a_ref[...] + bin_b_ref[...]) * (trial_a_ref[...] + trial_b_ref[...])
    tiles = [gram[i : i + SUB, lane : lane + rank] for lane in (0, rank) for i in range(0, rank // 2, SUB)]
    zero = jnp.zeros_like(tiles[0])
    for i, tile in enumerate(inverse_tiles(tiles)):
        out_ref[i * SUB : (i + 1) * SUB, :] = jnp.concatenate([tile, zero], axis=1)
        out_ref[rank + i * SUB : rank + (i + 1) * SUB, :] = jnp.concatenate([zero, tile], axis=1)


def solve_kernel(own_ref, other_ref, inverse_ref, solved_ref, squares_ref):
    rank = inverse_ref.shape[0] // 2
    solved = jnp.dot(own_ref[...] + other_ref[...], inverse_ref[...], preferred_element_type=jnp.float32, precision=EXACT)
    solved_ref[...] = solved
    squares = jnp.sum(solved * solved, axis=0, keepdims=True)
    squares = jnp.broadcast_to(squares, squares_ref.shape)
    squares_ref[...] = squares + pltpu.roll(squares, rank, 1)


def scale_kernel(count, solved_ref, one_ref, two_ref, three_ref, four_ref, out_ref, weights_ref):
    share, rank = out_ref.shape
    rows = share // 2
    squares = (one_ref[...] + two_ref[...]) + (three_ref[...] + four_ref[...])
    weights = jnp.sqrt(squares[:1] / count + 1e-06)
    weights_ref[...] = weights[:, :rank]
    mine = solved_ref[pl.ds(pl.multiple_of(lax.axis_index("tri") * rows, SUB), rows), :] / weights
    out_ref[:rows, :] = mine[:, :rank]
    out_ref[rows:, :] = mine[:, rank:]


def local(neur, tri, tensor, bin_factor, trial_factor):
    axes = ("neur", "tri", "bin")
    rank = bin_factor.shape[1]
    f32 = jnp.float32

    def exchange(value, partner):
        flat = lambda n, t, b: (n * tri + t) * 2 + b
        places = [(n, t, b) for n in range(neur) for t in range(tri) for b in range(2)]
        return lax.ppermute(value, axes, [(flat(*place), flat(*partner(*place))) for place in places])

    def swap(value, n, t, b):
        return exchange(value, lambda i, j, k: (i ^ n, j ^ t, k ^ b))

    rows = tensor.shape[0]
    held = rows // 4
    share = rows // (2 * tri)
    sent, trial_gram, kept, local_factor, wide = send_products(tri, tensor, bin_factor.T, trial_factor)
    got = swap(sent, 0, 0, 1)
    own = own_products(tri, kept, local_factor, wide)
    bin_a, bin_b = sent[held:], got[held:]
    stages = tri.bit_length() - 1
    trial_gram, own = lax.optimization_barrier((trial_gram, own))

    def cross(value, stage):
        return exchange(value, lambda n, t, b: (n, t ^ (1 << (stage + (b ^ parity(t, tri))) % stages), 1 - b))

    block = own + got[:held]
    for stage in range(stages - 1):
        trial_gram = added(trial_gram, cross(trial_gram, stage))
        block = block + cross(block, stage)
    trial_other = cross(trial_gram, stages - 1)
    other_block = cross(block, stages - 1)
    inside = pl.BlockSpec(memory_space=pltpu.VMEM)
    inverse = pl.pallas_call(
        inverse_kernel,
        in_specs=[inside] * 4,
        out_specs=inside,
        out_shape=pltpu.VMEM((2 * rank, 2 * rank), f32),
        cost_estimate=pl.CostEstimate(flops=10000000000, bytes_accessed=200000, transcendentals=0),
        name="inverse",
    )(*held_in(bin_a, bin_b, trial_gram, trial_other))
    solved, squares = pl.pallas_call(
        solve_kernel,
        in_specs=[inside] * 3,
        out_specs=(inside, inside),
        out_shape=(pltpu.VMEM((held, 2 * rank), f32), pltpu.VMEM((1, 2 * rank), f32)),
        name="solve",
    )(*held_in(block, other_block, inverse))
    squares = squares + swap(squares, 0, 0, 1)
    bit = 1
    parts = None
    while bit < neur:
        if bit * 2 < neur:
            far = exchange(squares, lambda n, t, b: (n ^ ((2 + b) * bit), t, b))
            near = swap(squares, bit, 0, 1)
            parts = [squares, near, far, swap(far, 0, 0, 1)]
            bit *= 4
        else:
            zero = jnp.zeros_like(squares)
            parts = [squares, swap(squares, bit, 0, 1), zero, zero]
            bit *= 2
        if bit < neur:
            squares = (parts[0] + parts[1]) + (parts[2] + parts[3])
    result, weights = pl.pallas_call(
        functools.partial(scale_kernel, rows * neur),
        in_specs=[inside] * 5,
        out_specs=(inside, inside),
        out_shape=(jax.ShapeDtypeStruct((share, rank), f32), jax.ShapeDtypeStruct((1, rank), f32)),
        name="scale",
    )(*held_in(solved, *parts))
    return (result, weights[0])


def solution(mesh):
    return jax.shard_map(
        functools.partial(local, mesh.shape["neur"], mesh.shape["tri"]),
        mesh=mesh,
        in_specs=(P("neur", "tri", "bin"), P("bin", None), P("tri", None)),
        out_specs=(P(("neur", "tri", "bin"), None), P()),
        check_vma=False,
    )
```
